512 devices in a mesh: band: 16 (over x, z_hi, core), col: 32 (over z_lo, y).
Axes of the slice: x: 4, y: 4, z: 16 (z_hi: 2, z_lo: 8; z = z_hi * 8 + z_lo), core: 2. Of those that a mesh axis runs over, the one named last changes fastest.
Arguments:
- left_image: bfloat16 [64, 4096, 256], P('band', 'col'), may hold values from -6 to 6
- right_image: bfloat16 [64, 4096, 256], P('band', 'col'), may hold values from -6 to 6
- kernel: bfloat16 [2304, 256], replicated, may hold values from -0.125 to 0.125
- valid_mask: int32 [64, 4096], P('band', 'col'), may hold values 0 or 1
- disparity: int32 [64, 4096], P('band', 'col'), may hold values from 0 to 511
Outputs:
- grad_left: bfloat16 [64, 4096, 256], P('band', 'col')
- grad_right: bfloat16 [64, 4096, 256], P('band', 'col')
The draws below stay inside these ranges and needn't reach their ends.
All inputs are finite; a program needn't handle non-finite values. No bound on the sum of `valid_mask` on one device may be relied on, other than what follows from the above.
Results may differ from the reference program's by a relative error of at most 0.011.
Values may be sent and summed in bfloat16 or wider, within the bound.
No kernel may reach another device: no remote copies, remote signals or barrier semaphores. Data moves between devices by JAX's collectives and lax.ppermute only.
A program may use at most 64 MiB of HBM per device.

```python
import jax
import jax.numpy as jnp
from jax import lax

C = 256
DISP = 512
COLS_DEV = 128
HEIGHT = 64
WIDTH = 4096


def plant(result, stream_key, smallest, top_value):
    longest = result.shape.index(max(result.shape))
    spots = []
    for shift in (0, 1):
        where = [jax.random.randint(jax.random.fold_in(stream_key, axis), (), 0, length) for axis, length in enumerate(result.shape)]
        where[longest] = (where[longest] + shift) % result.shape[longest]
        spots.append(tuple(where))
    return result.at[spots[0]].set(smallest).at[spots[1]].set(top_value)


def shard_levels(own_key, extent, shards, least, high):
    gain = 1.0
    for position, blocks in shards:
        steps = jax.random.uniform(jax.random.fold_in(jax.random.fold_in(own_key, 6), position), (blocks,), jnp.float32, least / len(shards), high / len(shards))
        gain = gain * jnp.repeat(jnp.exp(steps), extent[position] // blocks).reshape((-1,) + (1,) * (len(extent) - 1 - position))
    return gain


def bell_draw(key, extent, spread, reach, shards=(), kind=jnp.bfloat16):
    result = jax.random.normal(key, extent, jnp.float32) * spread
    if len(shards) > 0:
        result = shard_levels(key, extent, shards, -0.22, 0.18) * result
    return jnp.clip(result, min=-reach, max=reach).astype(kind)


def setup_inputs(seed: int = 0) -> dict:
    key_list = jax.random.split(jax.random.key(seed), 6)
    return {
        "left_image": bell_draw(key_list[0], (HEIGHT, WIDTH, C), 1.0, 6.0, ((0, 16), (1, 32))),
        "right_image": bell_draw(key_list[1], (HEIGHT, WIDTH, C), 1.0, 6.0, ((0, 16), (1, 32))),
        "kernel": bell_draw(key_list[2], (9 * C, C), (9 * C) ** -0.5, 0.125),
        "valid_mask": plant((jax.random.randint(key_list[3], (HEIGHT, WIDTH), 0, 4) < 3).astype(jnp.int32), jax.random.fold_in(key_list[3], 1), 0, 1),
        "disparity": plant(jax.random.randint(key_list[4], (HEIGHT, WIDTH), 0, DISP), jax.random.fold_in(key_list[4], 1), 0, DISP - 1).astype(jnp.int32),
    }


def conv_image(image_in, weights):
    height = image_in.shape[0]
    columns = image_in.shape[1]
    padded = jnp.pad(image_in, ((1, 1), (1, 1), (0, 0)))

    def one_row(row_index):
        window = lax.dynamic_slice_in_dim(padded, row_index, 3, 0)
        pieces = [window[row_off, col_off:col_off + columns] for row_off in range(3) for col_off in range(3)]
        patches = jnp.concatenate(pieces, axis=1)
        return jnp.dot(patches, weights, preferred_element_type=jnp.float32)

    return lax.map(one_row, jnp.arange(height, dtype=jnp.int32))


def flip_kernel(kernel):
    blocks = kernel.reshape(3, 3, C, C)[::-1, ::-1]
    return jnp.transpose(blocks, (0, 1, 3, 2)).reshape(9 * C, C)


def row_terms(left_row, right_row, mask_row, truth_row):
    columns = left_row.shape[0]
    right_pad = jnp.concatenate([jnp.zeros((DISP, C), right_row.dtype), right_row], 0)
    disparities = jnp.arange(DISP, dtype=jnp.int32)
    inner = jnp.arange(COLS_DEV, dtype=jnp.int32)
    lookup = inner[:, None] + DISP - disparities[None, :]
    factor = C ** -0.5

    def column_block(running, offset):
        left_block = lax.dynamic_slice_in_dim(left_row, offset, COLS_DEV, 0)
        segment = lax.dynamic_slice_in_dim(right_pad, offset, COLS_DEV + DISP, 0)
        scores = jnp.dot(left_block, segment.T, preferred_element_type=jnp.float32) * factor
        correlation = jnp.take_along_axis(scores, lookup, axis=1)
        validity = lax.dynamic_slice_in_dim(mask_row, offset, COLS_DEV, 0).astype(jnp.float32)
        truth_block = lax.dynamic_slice_in_dim(truth_row, offset, COLS_DEV, 0)
        distance = (disparities[None, :] - truth_block[:, None]).astype(jnp.float32)
        target = jnp.exp(-distance * distance / 8.0)
        gradient = (validity[:, None] * (correlation - target) * (C / DISP)).astype(jnp.bfloat16)
        banded = jnp.zeros((COLS_DEV, COLS_DEV + DISP), gradient.dtype).at[inner[:, None], lookup].set(gradient)
        left_term = jnp.dot(banded, segment, preferred_element_type=jnp.float32) * factor
        right_term = jnp.dot(banded.T, left_block, preferred_element_type=jnp.float32) * factor
        current = lax.dynamic_slice_in_dim(running, offset, COLS_DEV + DISP, 0)
        running = lax.dynamic_update_slice_in_dim(running, current + right_term, offset, 0)
        return running, left_term

    offsets = jnp.arange(0, columns, COLS_DEV, dtype=jnp.int32)
    initial = jnp.zeros((DISP + columns, C), jnp.float32)
    right_sum, left_parts = lax.scan(column_block, initial, offsets)
    return left_parts.reshape(columns, C), right_sum[DISP:]


def reference(left_image, right_image, kernel, valid_mask, disparity):
    left_feat = conv_image(left_image, kernel).astype(jnp.bfloat16)
    right_feat = conv_image(right_image, kernel).astype(jnp.bfloat16)

    def one_row(items):
        return row_terms(items[0], items[1], items[2], items[3])

    dleft, dright = lax.map(one_row, (left_feat, right_feat, valid_mask, disparity))
    flipped = flip_kernel(kernel)
    grad_left = conv_image(dleft.astype(jnp.bfloat16), flipped).astype(jnp.bfloat16)
    grad_right = conv_image(dright.astype(jnp.bfloat16), flipped).astype(jnp.bfloat16)
    return grad_left, grad_right
```

```python
import functools

import jax
import jax.numpy as jnp
from jax import lax
from jax.experimental import pallas as pl
from jax.experimental.pallas import tpu as pltpu
from jax.sharding import PartitionSpec as P

DISP = 512
COLS = 128
PAD = 16
WIDE = COLS + PAD
REACH = DISP // COLS
BF16 = jnp.bfloat16
F32 = jnp.float32
VMEM_LIMIT = 48 * 1024 * 1024


def rows_of(refs, image, table, rows):
    return jnp.concatenate([refs[table[row][0]][image, table[row][1]] for row in rows], 0)


def conv_sums(refs, image, table, rows, w_ref, odd, back):
    taps = []
    for col in range(3):
        total = None
        for row in range(3):
            inputs = rows_of(refs, image, table, [r + row - 1 for r in rows])
            if back:
                w_row = jnp.where(odd == 1, row, 2 - row)
                weights = w_ref[w_row * 3 + (2 - col)]
                dims = (((1,), (1,)), ((), ()))
            else:
                w_row = jnp.where(odd == 1, 2 - row, row)
                weights = w_ref[w_row * 3 + col]
                dims = (((1,), (0,)), ((), ()))
            part = lax.dot_general(inputs, weights, dims, preferred_element_type=F32)
            total = part if total is None else total + part
        taps.append(total)
    results = []
    for index in range(len(rows)):
        low, mid, high = (tap[index * WIDE : (index + 1) * WIDE] for tap in taps)
        low = pltpu.roll(low, 1, 0)
        high = pltpu.roll(high, WIDE - 1, 0)
        results.append((low + mid + high)[:COLS])
    return results


def feature_kernel(table, rows, count, *args):
    odd_ref, refs, w_ref = args[0], args[1 : 1 + count], args[1 + count]
    left_ref, right_ref = args[2 + count :]
    odd = odd_ref[0]
    lefts = conv_sums(refs, 0, table, rows, w_ref, odd, False)
    rights = conv_sums(refs, 1, table, rows, w_ref, odd, False)
    slot = lax.broadcasted_iota(jnp.int32, (PAD, 256), 0)
    for index, row in enumerate(rows):
        array, place = table[row]
        code = refs[array][0, place, COLS:].astype(F32)
        code = jnp.where(slot == 1, code, 0.0)
        left, right = lefts[index], rights[index]
        left_ref[index, :COLS] = left.astype(BF16)
        right_ref[index, :COLS] = right.astype(BF16)
        left_ref[index, COLS:] = jnp.where(slot == 0, right[0:1], code).astype(BF16)
        right_ref[index, COLS:] = jnp.where(slot == 0, left[COLS - 1 : COLS], code).astype(BF16)


def grad_kernel(table, rows, count, *args):
    odd_ref, refs, w_ref = args[0], args[1 : 1 + count], args[1 + count]
    outs = args[2 + count :]
    odd = odd_ref[0]
    for image in range(2):
        results = conv_sums(refs, image, table, rows, w_ref, odd, True)
        for index, row in enumerate(rows):
            outs[image][jnp.where(odd == 1, 3 - row, row)] = results[index].astype(BF16)


def vmem_specs(count):
    return [pl.BlockSpec(memory_space=pltpu.VMEM)] * count


def conv_cost(rows):
    return pl.CostEstimate(
        flops=2 * 2 * rows * WIDE * 2304 * 256, bytes_accessed=2 * 2**20, transcendentals=0
    )


def feature_rows(odd, arrays, table, rows, weights):
    shape = jax.ShapeDtypeStruct((len(rows), WIDE, 256), BF16)
    return pl.pallas_call(
        functools.partial(feature_kernel, table, rows, len(arrays)),
        out_shape=(shape, shape),
        in_specs=[pl.BlockSpec(memory_space=pltpu.SMEM)] + vmem_specs(len(arrays) + 1),
        out_specs=tuple(vmem_specs(2)),
        compiler_params=pltpu.CompilerParams(vmem_limit_bytes=VMEM_LIMIT),
        cost_estimate=conv_cost(len(rows)),
        name="features",
    )(odd, *arrays, weights)


def grad_rows(odd, arrays, table, rows, weights):
    shape = jax.ShapeDtypeStruct((4, COLS, 256), BF16)
    return pl.pallas_call(
        functools.partial(grad_kernel, table, rows, len(arrays)),
        out_shape=(shape, shape),
        in_specs=[pl.BlockSpec(memory_space=pltpu.SMEM)] + vmem_specs(len(arrays) + 1),
        out_specs=tuple(vmem_specs(2)),
        compiler_params=pltpu.CompilerParams(vmem_limit_bytes=VMEM_LIMIT),
        cost_estimate=conv_cost(len(rows)),
        name="grads",
    )(odd, *arrays, weights)


def decoded(code):
    low = code[:, COLS:]
    return code[:, :COLS] * 16.0 + low - 1.0, jnp.where(low > 0.5, 0.5, 0.0)


def upright(row):
    return jnp.swapaxes(jnp.broadcast_to(row, (COLS, COLS)), 0, 1)


def gradient(scores, delta, disparity, half_mask):
    inside = jnp.abs(delta - (DISP / 2 - 0.5)) < DISP / 2
    off = delta - disparity
    target = jnp.exp(off * off * (-1.0 / 8.0))
    return jnp.where(inside, half_mask * (scores * (1.0 / 16.0) - target), 0.0).astype(BF16)


def match_kernel(count, *args):
    inner_ref, left_ref, right_ref = args[:3]
    from_left, from_right = args[3 : 3 + REACH], args[3 + REACH : 3 + 2 * REACH]
    out_ref = args[3 + 2 * REACH]
    inner = inner_ref[0].astype(F32)
    slot = lax.broadcasted_iota(jnp.int32, (PAD, 256), 0)
    place = lax.broadcasted_iota(jnp.int32, (WIDE, COLS), 0)
    place = jnp.where(place == WIDE - 1, -1, jnp.where(place > COLS, -(2**16), place))
    place = place.astype(F32)
    lane = lax.broadcasted_iota(jnp.int32, (WIDE, COLS), 1).astype(F32)
    ahead = place - lane
    nt = (((1,), (1,)), ((), ()))
    nn = (((1,), (0,)), ((), ()))
    for row in range(count):
        codes = [decoded(left_ref[row, COLS:].astype(F32)[1:2])]
        codes += [decoded(ref[row, COLS:].astype(F32)[1:2]) for ref in from_right]
        before = decoded(from_left[0][row, COLS:].astype(F32)[1:2])
        rights = [from_left[k - 1][row, :COLS] for k in range(REACH, 0, -1)]
        rights.append(right_ref[row, :COLS])
        lefts = [left_ref[row, :COLS]] + [ref[row, :COLS] for ref in from_right]
        right_cat = jnp.concatenate(rights, 0)
        left_cat = jnp.concatenate(lefts, 0)
        left_after = from_right[0][row, 0:PAD].astype(F32)[0:1]
        left_before = from_left[0][row, COLS:].astype(F32)[0:1]
        right_after = from_right[0][row, COLS:].astype(F32)[0:1]
        right_before = from_left[0][row, COLS - PAD : COLS].astype(F32)[PAD - 1 : PAD]
        left_side = jnp.where(
            slot == 0, left_after, jnp.where(slot == PAD - 1, left_before, 0.0)
        )
        right_side = jnp.where(
            slot == 0, right_after, jnp.where(slot == PAD - 1, right_before, 0.0)
        )
        left_wide = jnp.concatenate([lefts[0], left_side.astype(BF16)], 0)
        right_wide = jnp.concatenate([rights[-1], right_side.astype(BF16)], 0)
        side = slot[:, :COLS]
        disparities, masks = [], []
        for which, parts in ((0, disparities), (1, masks)):
            main = upright(codes[0][which])
            beside = jnp.where(
                side == 0,
                codes[1][which][:, 0:1],
                jnp.where(side == PAD - 1, before[which][:, COLS - 1 : COLS], 0.0),
            )
            parts.append(jnp.concatenate([main, beside], 0))
        scores = lax.dot_general(left_wide, right_cat, nt, preferred_element_type=F32)
        grads = []
        for block in range(REACH + 1):
            tile = scores[:, block * COLS : (block + 1) * COLS]
            delta = ahead + float((REACH - block) * COLS)
            grads.append(gradient(tile, delta, disparities[0], masks[0]))
        left_grad = lax.dot_general(
            jnp.concatenate(grads, 1), right_cat, nn, preferred_element_type=F32
        )
        single = jnp.sum(left_after * right_after, 1, keepdims=True)
        weight = gradient(single, jnp.zeros_like(single), codes[1][0][:, 0:1], codes[1][1][:, 0:1])
        extra = jnp.where(slot == 0, weight.astype(F32) * right_after, 0.0)
        out_ref[0, row, :COLS] = (left_grad[:COLS] * (1.0 / 16.0)).astype(BF16)
        out_ref[0, row, COLS:] = ((left_grad[COLS:] + extra) * (1.0 / 16.0)).astype(BF16)
        scores = lax.dot_general(right_wide, left_cat, nt, preferred_element_type=F32)
        grads = []
        for block in range(REACH + 1):
            tile = scores[:, block * COLS : (block + 1) * COLS]
            delta = float(block * COLS) - ahead
            grads.append(gradient(tile, delta, codes[block][0], codes[block][1]))
        right_grad = lax.dot_general(
            jnp.concatenate(grads, 1), left_cat, nn, preferred_element_type=F32
        )
        single = jnp.sum(left_before * right_before, 1, keepdims=True)
        weight = gradient(
            single,
            jnp.zeros_like(single),
            before[0][:, COLS - 1 : COLS],
            before[1][:, COLS - 1 : COLS],
        )
        extra = jnp.where(slot == PAD - 1, weight.astype(F32) * left_before, 0.0)
        keep = jnp.where(slot == PAD - 1, inner, 1.0)
        out_ref[1, row, :COLS] = (right_grad[:COLS] * (1.0 / 16.0)).astype(BF16)
        out_ref[1, row, COLS:] = ((right_grad[COLS:] + extra) * (1.0 / 16.0) * keep).astype(BF16)


def match_rows(inner, left, right, from_left, from_right):
    count = left.shape[0]
    return pl.pallas_call(
        functools.partial(match_kernel, count),
        out_shape=jax.ShapeDtypeStruct((2, count, WIDE, 256), BF16),
        in_specs=[pl.BlockSpec(memory_space=pltpu.SMEM)] + vmem_specs(2 + 2 * REACH),
        out_specs=pl.BlockSpec(memory_space=pltpu.VMEM),
        compiler_params=pltpu.CompilerParams(vmem_limit_bytes=VMEM_LIMIT),
        cost_estimate=pl.CostEstimate(
            flops=8 * count * WIDE * 640 * 256,
            bytes_accessed=count * 2**20,
            transcendentals=2 * count * WIDE * 640,
        ),
        name="match",
    )(inner, left, right, *from_left, *from_right)


def shifted(value, steps):
    count = lax.axis_size("col")
    pairs = [(i, i + steps) for i in range(count) if 0 <= i + steps < count]
    return lax.ppermute(value, "col", pairs)


def exchanged(left, right):
    from_left = [shifted(right, step) for step in range(1, REACH + 1)]
    from_right = [shifted(left, -step) for step in range(1, REACH + 1)]
    return from_left, from_right


def shards(left_image, right_image, kernel, valid_mask, disparity):
    bands = lax.axis_size("band")
    odd = lax.axis_index("band") % 2
    odd_arg = odd.astype(jnp.int32).reshape(1)
    inner_arg = (lax.axis_index("col") > 0).astype(jnp.int32).reshape(1)
    weights = kernel.reshape(9, 256, 256)
    far_pairs = [(i, i + 1) for i in range(1, bands - 1, 2)]
    far_pairs += [(target, source) for source, target in far_pairs]
    near_pairs = [(i, i ^ 1) for i in range(bands)]

    stacked = jnp.stack((left_image, right_image), 0)
    own = jnp.where(odd == 1, stacked[:, ::-1], stacked)
    code = jnp.concatenate(
        [disparity >> 4, jnp.where(valid_mask > 0, (disparity & 15) + 1, 0)], 1
    ).astype(BF16)
    code = jnp.where(odd == 1, code[::-1], code)

    low = shifted(own[:, :, COLS - 1 :], 1)
    high = shifted(own[:, :, :1], -1)
    code = jnp.broadcast_to(code[None, :, None], (2, 4, 1, 256))
    blank = jnp.zeros((2, 4, PAD - 3, 256), BF16)
    own = jnp.concatenate([own, high, code, blank, low], 2)

    far = lax.ppermute(own[:, :2], "band", far_pairs)
    near = lax.ppermute(own[:, 3:], "band", near_pairs)

    table = {row: (0, row) for row in range(4)}
    left, right = feature_rows(
        odd_arg, (own, near), {**table, 4: (1, 0)}, (1, 2, 3), weights
    )
    inside = match_rows(inner_arg, left, right, *exchanged(left, right))
    near_grad = lax.ppermute(inside[:, 2:], "band", near_pairs)

    left, right = feature_rows(
        odd_arg, (own, far), {**table, -1: (1, 0), -2: (1, 1)}, (-1, 0), weights
    )
    edge = match_rows(inner_arg, left, right, *exchanged(left, right))

    grads = {-1: (0, 0), 0: (0, 1), 1: (1, 0), 2: (1, 1), 3: (1, 2), 4: (2, 0)}
    return grad_rows(odd_arg, (edge, inside, near_grad), grads, (0, 1, 2, 3), weights)


def solution(mesh):
    return jax.shard_map(
        shards,
        mesh=mesh,
        in_specs=(
            P("band", "col", None),
            P("band", "col", None),
            P(),
            P("band", "col"),
            P("band", "col"),
        ),
        out_specs=(P("band", "col", None), P("band", "col", None)),
        check_vma=False,
    )
```
